32 devices in a mesh: bead: 8 (over y, x, core), space: 4 (over z).
Axes of the slice: x: 2, y: 2, z: 4, core: 2. Of those that a mesh axis runs over, the one named last changes fastest.
Arguments:
- positions: float32 [32, 3, 2048], P('bead', None, 'space'), may hold values from -3 to 3
- momenta: float32 [32, 3, 2048], P('bead', None, 'space'), may hold values from -6 to 6
- neighbours: int32 [32, 2048], P(None, 'space'), may hold values from 0 to 767, as said below
- ghost_rows: int32 [1024], P('space'), may hold values from 0 to 511
- species: int32 [2048], P('space'), may hold values from 0 to 1
- species_scale: float32 [2], replicated, may hold values from 0.5 to 2
- mass_table: float32 [2], replicated, may hold values from 0.25 to 1
- w_in: float32 [128, 8], replicated, may hold values from -2 to 2
- w_out: float32 [8, 128], replicated, may hold values from -0.5 to 0.5
Outputs:
- new_positions: float32 [32, 3, 2048], P('bead', None, 'space')
- new_momenta: float32 [32, 3, 2048], P('bead', None, 'space')
The draws below stay inside these ranges and needn't reach their ends.
Inputs may be any that keep to these rules, and one draw needn't show every extreme that they name: `neighbours`: A neighbour entry indexes the window of its atom's domain; slots beyond an atom's live count hold the atom's own position 128 + (atom index mod 512); every atom has at least 8 live slots. `ghost_rows`: domain d's block is entries 2 * 128 * d to 2 * 128 * (d + 1) - 1; entries index atoms within domain d.
All inputs are finite; a program needn't handle non-finite values.
Results may differ from the reference program's by a relative error of at most 0.0003.
Values sent between devices are 32-bit elements; how exact they have to be, the bound alone decides.
A program may use at most 64 MiB of HBM per device.

```python
import math
import jax
import jax.numpy as jnp
import numpy as np
from jax import lax

BEADS = 32
CB = 4
SPECIES = 2
H = 128
NRBF = 8
SLOTS = 32
NINNER = 3
ATOM_DEV = 512
GHOST = 128
ATOMS = 2048
GHOST_ROWS = 1024
N_SPACE = 4


def draw_neighbours(key, part):
    first_key = jax.random.fold_in(key, 11)
    second_key = jax.random.fold_in(key, 23)
    counts = jax.random.randint(first_key, (1, ATOMS), SLOTS // 4, SLOTS + 1)
    picks = jax.random.randint(second_key, (SLOTS, ATOMS), 0, ATOM_DEV + 2 * GHOST)
    slot_ids = jnp.arange(SLOTS, dtype=jnp.int32)[:, None]
    itself = GHOST + jnp.arange(ATOMS, dtype=jnp.int32) % ATOM_DEV
    return jnp.where(slot_ids < counts, picks, itself[None, :]).astype(jnp.int32)


def touch_ends(entries, stream_key, least, high):
    extent = entries.shape
    index_at = [jax.random.randint(jax.random.fold_in(stream_key, axis), (), 0, extent[axis]) for axis in range(len(extent))]
    entries = entries.at[tuple(index_at)].set(least)
    longest = extent.index(max(extent))
    index_at[longest] = (index_at[longest] + 1) % extent[longest]
    return entries.at[tuple(index_at)].set(high)


def levels(key, extent, split, smallest, largest):
    factor_of = 1.0
    for axis_at, shards_of in split:
        steps = jax.random.uniform(jax.random.fold_in(jax.random.fold_in(key, 6), axis_at), (shards_of,), jnp.float32, smallest / len(split), largest / len(split))
        factor_of = factor_of * jnp.repeat(jnp.exp(steps), extent[axis_at] // shards_of).reshape((-1,) + (1,) * (len(extent) - 1 - axis_at))
    return factor_of


def bell_draw(own_key, shape, width, bound, pieces=(), held_as=jnp.bfloat16):
    drawn = width * jax.random.normal(own_key, shape, jnp.float32)
    if pieces:
        drawn = drawn * levels(own_key, shape, pieces, -0.22, 0.18)
    return jnp.clip(drawn, -bound, bound).astype(held_as)


def setup_inputs(seed: int = 0) -> dict:
    key_list = jax.random.split(jax.random.key(seed), 10)
    positions = bell_draw(key_list[0], (BEADS, 3, ATOMS), 0.5, 3.0, ((0, 8), (2, 4)), jnp.float32)
    momenta = bell_draw(key_list[1], (BEADS, 3, ATOMS), 1.0, 6.0, ((0, 8), (2, 4)), jnp.float32)
    neighbours = draw_neighbours(jax.random.fold_in(key_list[9], 71), 0)
    ghost_rows = touch_ends(jax.random.randint(key_list[3], (GHOST_ROWS,), 0, ATOM_DEV), jax.random.fold_in(key_list[3], 1), 0, ATOM_DEV - 1).astype(jnp.int32)
    species = touch_ends(jax.random.randint(key_list[4], (ATOMS,), 0, SPECIES), jax.random.fold_in(key_list[4], 1), 0, SPECIES - 1).astype(jnp.int32)
    species_scale = jnp.clip(jnp.exp(jax.random.uniform(key_list[5], (SPECIES,), jnp.float32, math.log(0.5), math.log(2.0))), 0.5, 2.0)
    mass_table = jnp.clip(jnp.exp(jax.random.uniform(key_list[6], (SPECIES,), jnp.float32, math.log(0.25), math.log(1.0))), 0.25, 1.0)
    w_in = bell_draw(key_list[7], (H, NRBF), NRBF ** -0.5, 2.0, (), jnp.float32)
    w_out = bell_draw(key_list[8], (NRBF, H), H ** -0.5, 0.5, (), jnp.float32)
    return dict(positions=positions, momenta=momenta, neighbours=neighbours, ghost_rows=ghost_rows, species=species, species_scale=species_scale, mass_table=mass_table, w_in=w_in, w_out=w_out)


polymer_freq = 10.0
outer_step = 6.0
pair_width = 1.0
pair_strength = 1.0
highest = lax.Precision.HIGHEST

def mode_matrix(count):
    beadpos = np.arange(count)[None, :]
    modeidx = np.arange(count)[:, None]
    middle = count // 2
    cosine = np.sqrt(2.0 / count) * np.cos(2.0 * np.pi * beadpos * modeidx / count)
    sine_rows = np.sqrt(2.0 / count) * np.sin(2.0 * np.pi * beadpos * modeidx / count)
    matrix = np.where(modeidx < middle, cosine, sine_rows)
    matrix = np.where(modeidx == 0, 1.0 / np.sqrt(count), matrix)
    matrix = np.where(modeidx == middle, np.cos(np.pi * beadpos) / np.sqrt(count), matrix)
    return matrix

def mode_scales(count, inner_step):
    frequency = 2.0 * polymer_freq * np.sin(np.pi * np.arange(count) / count)
    nonzero = np.where(frequency > 0, frequency, 1.0)
    cosine = np.cos(frequency * inner_step)
    drift_gain = np.where(frequency > 0, np.sin(frequency * inner_step) / nonzero, inner_step)
    spring = frequency * np.sin(frequency * inner_step)
    return (cosine, drift_gain, spring)

def polymer_tables(count, inner_step):
    modes = mode_matrix(count)
    cosine, drift_gain, spring = mode_scales(count, inner_step)
    persist = modes.T @ (cosine[:, None] * modes)
    coupling = modes.T @ (drift_gain[:, None] * modes)
    restoring = -(modes.T @ (spring[:, None] * modes))
    return (jnp.asarray(persist, jnp.float32), jnp.asarray(coupling, jnp.float32), jnp.asarray(restoring, jnp.float32))

def contraction(count, fewer):
    full_modes = mode_matrix(count)
    small_modes = mode_matrix(fewer)
    kept = list(range(fewer // 2 + 1)) + list(range(count - fewer // 2 + 1, count))
    contract = np.sqrt(fewer / count) * (small_modes.T @ full_modes[kept])
    expand = count / fewer * contract.T
    return (jnp.asarray(contract, jnp.float32), jnp.asarray(expand, jnp.float32))

def radial_rates(count):
    return 0.2 * 2.0 ** (np.arange(count) / 2.0)

def species_lookup(species, table):
    kinds = jnp.arange(table.shape[0], dtype=jnp.int32)
    return lax.optimization_barrier(jnp.sum(jnp.where(species[None, :] == kinds[:, None], table[:, None], 0.0), axis=0))

def pair_forces(extended, targets, centres):
    others = extended[:, targets]
    middle = extended[:, centres]
    offsets = others[:3] - middle[:3, None, :]
    squared = lax.optimization_barrier(jnp.sum(offsets * offsets, axis=0))
    weights = others[3] * jnp.exp(-squared / pair_width)
    return pair_strength * middle[3] * lax.optimization_barrier(jnp.sum(weights[None] * offsets, axis=1))

def learned_forces(extended, charges, targets, centres, w_in, w_out):
    live = (targets != centres[None, :]).astype(jnp.float32)
    weights = charges[targets] * live
    others = extended[:, targets]
    middle = extended[:, centres]
    offsets = others - middle[:, None, :]
    squared = lax.optimization_barrier(jnp.sum(offsets * offsets, axis=0))
    rates = jnp.asarray(radial_rates(w_in.shape[1]), jnp.float32)
    basis = jnp.exp(-rates[:, None, None] * squared[None])
    message = lax.optimization_barrier(jnp.sum(weights[None] * basis, axis=1)) / targets.shape[0]
    hidden = jax.nn.silu(jnp.dot(w_in, message, precision=highest, preferred_element_type=jnp.float32))
    radial = jnp.dot(w_out, hidden, precision=highest, preferred_element_type=jnp.float32)
    profile = lax.optimization_barrier(jnp.sum(radial[:, None, :] * basis, axis=0))
    return lax.optimization_barrier(jnp.sum((weights * profile)[None] * offsets, axis=1))

def window(values, ghost_rows):
    channels = values.shape[0]
    blocks = values.reshape(channels, N_SPACE, ATOM_DEV)
    picked = ghost_rows.reshape(N_SPACE, 2 * GHOST)
    sends = jnp.take_along_axis(blocks, jnp.broadcast_to(picked[None], (channels, N_SPACE, 2 * GHOST)), axis=2)
    from_below = jnp.roll(sends[:, :, GHOST:], 1, axis=1)
    from_above = jnp.roll(sends[:, :, :GHOST], -1, axis=1)
    return jnp.concatenate([from_below, blocks, from_above], axis=2).reshape(channels, -1)

def reference(positions, momenta, neighbours, ghost_rows, species, species_scale, mass_table, w_in, w_out):
    inner_step = outer_step / NINNER
    persist, coupling, restoring = polymer_tables(BEADS, inner_step)
    contract, expand = contraction(BEADS, CB)
    charges = species_lookup(species, species_scale)
    masses = species_lookup(species, mass_table)
    window_length = ATOM_DEV + 2 * GHOST
    atom_ids = jnp.arange(ATOMS, dtype=jnp.int32)
    domain = atom_ids // ATOM_DEV
    targets = domain[None, :] * window_length + neighbours
    centres = domain * window_length + GHOST + atom_ids % ATOM_DEV
    charge_window = window(charges[None], ghost_rows)[0]

    def cheap_forces(coords):

        def single(bead_coords):
            extended = window(jnp.concatenate([bead_coords, charges[None]], axis=0), ghost_rows)
            return pair_forces(extended, targets, centres)
        return lax.map(single, coords)

    def expensive_forces(coords):
        reduced = jnp.einsum('cb,bxa->cxa', contract, coords, precision=highest)

        def single(reduced_coords):
            return learned_forces(window(reduced_coords, ghost_rows), charge_window, targets, centres, w_in, w_out)
        return jnp.einsum('bc,cxa->bxa', expand, lax.map(single, reduced), precision=highest)

    def propagate(coords, moments):
        new_coords = jnp.einsum('ab,bxn->axn', persist, coords, precision=highest) + jnp.einsum('ab,bxn->axn', coupling, moments, precision=highest) / masses
        new_moments = jnp.einsum('ab,bxn->axn', persist, moments, precision=highest) + jnp.einsum('ab,bxn->axn', restoring, coords, precision=highest) * masses
        return (new_coords, new_moments)
    coords = positions
    moments = momenta + 0.5 * outer_step * expensive_forces(coords)
    cheap_now = cheap_forces(coords)
    for repeat in range(NINNER):
        moments = moments + 0.5 * inner_step * cheap_now
        coords, moments = propagate(coords, moments)
        cheap_now = cheap_forces(coords)
        moments = moments + 0.5 * inner_step * cheap_now
    moments = moments + 0.5 * outer_step * expensive_forces(coords)
    return (coords, moments)
```

```python
import jax
import jax.numpy as jnp
import numpy as np
from jax import lax
from jax.experimental import pallas as pl
from jax.experimental.pallas import tpu as pltpu
from jax.sharding import PartitionSpec as P

BEADS = 32
CB = 4
NINNER = 3


polymer_freq = 10.0
outer_step = 6.0
pair_width = 1.0
pair_strength = 1.0
highest = lax.Precision.HIGHEST


def mode_matrix(count):
    beadpos = np.arange(count)[None, :]
    modeidx = np.arange(count)[:, None]
    middle = count // 2
    cosine = np.sqrt(2.0 / count) * np.cos(2.0 * np.pi * beadpos * modeidx / count)
    sine_rows = np.sqrt(2.0 / count) * np.sin(2.0 * np.pi * beadpos * modeidx / count)
    matrix = np.where(modeidx < middle, cosine, sine_rows)
    matrix = np.where(modeidx == 0, 1.0 / np.sqrt(count), matrix)
    matrix = np.where(modeidx == middle, np.cos(np.pi * beadpos) / np.sqrt(count), matrix)
    return matrix


def mode_scales(count, inner_step):
    frequency = 2.0 * polymer_freq * np.sin(np.pi * np.arange(count) / count)
    nonzero = np.where(frequency > 0, frequency, 1.0)
    cosine = np.cos(frequency * inner_step)
    drift_gain = np.where(frequency > 0, np.sin(frequency * inner_step) / nonzero, inner_step)
    spring = frequency * np.sin(frequency * inner_step)
    return (cosine, drift_gain, spring)


def contraction(count, fewer):
    full_modes = mode_matrix(count)
    small_modes = mode_matrix(fewer)
    kept = list(range(fewer // 2 + 1)) + list(range(count - fewer // 2 + 1, count))
    contract = np.sqrt(fewer / count) * (small_modes.T @ full_modes[kept])
    expand = count / fewer * contract.T
    return (contract, expand)


def radial_rates(count):
    return 0.2 * 2.0 ** (np.arange(count) / 2.0)

LANES = 128
TILE = 8
MESH = pl.DeviceIdType.MESH


def tables(devices, per_device):
    inner_step = outer_step / NINNER
    modes = mode_matrix(BEADS)
    cosine, drift_gain, spring = mode_scales(BEADS, inner_step)
    persist = modes.T @ (cosine[:, None] * modes)
    coupling = modes.T @ (drift_gain[:, None] * modes)
    restoring = -(modes.T @ (spring[:, None] * modes))
    contract, expand = contraction(BEADS, CB)
    rows = -(-6 * per_device // TILE) * TILE
    full = devices * rows
    blocks = ((persist, coupling), (restoring, persist))

    def places(component, kind):
        bead = np.arange(BEADS)
        local = component * 2 * per_device + kind * per_device + bead % per_device
        return bead // per_device * rows + local

    move = np.zeros((full, full))
    reduce = np.zeros((CB, TILE, full))
    spread = np.zeros((full, CB * TILE))
    for component in range(3):
        for out in range(2):
            for kind in range(2):
                move[np.ix_(places(component, out), places(component, kind))] = blocks[out][kind]
        for member in range(CB):
            reduce[member, component, places(component, 0)] = contract[member]
            spread[places(component, 1), member * TILE + component] = (
                0.5 * outer_step * expand[:, member]
            )
    reduce_moved = reduce @ move
    move_spread = move @ spread
    share = reduce.reshape(CB * TILE, devices, rows).transpose(1, 0, 2)
    found = (
        move.reshape(devices, rows, full),
        share,
        reduce_moved,
        spread.reshape(devices, rows, CB * TILE),
        move_spread.reshape(devices, rows, CB * TILE),
    )
    return tuple(jnp.asarray(table, jnp.float32) for table in found)


def dot(a, b):
    return jnp.dot(a, b, precision=highest, preferred_element_type=jnp.float32)


def pick(chunks, low, high):
    found = None
    for number, chunk in enumerate(chunks):
        value = jnp.take_along_axis(chunk, low, axis=1, mode="promise_in_bounds")
        found = value if found is None else jnp.where(high == number, value, found)
    return found


def cycle_kernel(
    pos_ref, mom_ref, near_ref, ghost_ref, species_ref, scale_ref, mass_ref, w_in_ref, w_out_ref,
    move_ref, share_ref, moved_ref, spread_ref, mspread_ref,
    new_pos_ref, new_mom_ref,
    state, kick, weight, gathered, ghost_out, ghost_in, part_out, part_in, whole,
    qghost_out, qghost_in, piece,
    part_s, part_r, ghost_s, ghost_r, qghost_s, qghost_r, all_s, all_r, piece_s, piece_r,
):
    per_device, _, atoms = pos_ref.shape
    slots = near_ref.shape[0]
    rows = state.shape[1]
    ghosts = ghost_ref.shape[1]
    devices = lax.axis_size("bead")
    domains = lax.axis_size("space")
    me = lax.axis_index("bead")
    domain = lax.axis_index("space")
    above = lax.rem(domain + 1, domains)
    below = lax.rem(domain + domains - 1, domains)
    peers = [lax.rem(me + j, devices) for j in range(devices)]
    senders = [lax.rem(me + devices - j, devices) for j in range(devices)]
    inner_step = outer_step / NINNER
    groups = devices // CB
    share = atoms // groups
    cover = piece.shape[3]
    member = me // groups
    first = lax.rem(me, groups) * share // LANES * LANES
    ghost_chunks = ghosts // LANES
    atom_chunks = atoms // LANES

    barrier = pltpu.get_barrier_semaphore()
    for j in range(1, devices):
        pl.semaphore_signal(barrier, inc=1, device_id={"bead": peers[j]}, device_id_type=MESH)
    for target in (above, below):
        pl.semaphore_signal(barrier, inc=1, device_id={"space": target}, device_id_type=MESH)

    def to_peer(src, dst, send, recv, j):
        return pltpu.make_async_remote_copy(
            src_ref=src, dst_ref=dst, send_sem=send.at[j], recv_sem=recv.at[j],
            device_id={"bead": peers[j]}, device_id_type=MESH,
        )

    def to_side(src, dst, send, recv, side):
        return pltpu.make_async_remote_copy(
            src_ref=src, dst_ref=dst, send_sem=send.at[side], recv_sem=recv.at[side],
            device_id={"space": (above, below)[side]}, device_id_type=MESH,
        )

    def row_of(component, kind, bead):
        return (component * 2 + kind) * per_device + bead

    species = species_ref[...]
    charge = jnp.zeros((1, atoms), jnp.float32)
    mass = jnp.zeros((1, atoms), jnp.float32)
    for kind in range(scale_ref.shape[0]):
        charge = jnp.where(species == kind, scale_ref[kind], charge)
        mass = jnp.where(species == kind, mass_ref[kind], mass)
    inverse = 1.0 / mass

    kick[...] = jnp.zeros(kick.shape, jnp.float32)
    if rows > 6 * per_device:
        state[0] = jnp.zeros((rows, atoms), jnp.float32)
    for component in range(3):
        for bead in range(per_device):
            at = row_of(component, 0, bead)
            state[0, at : at + 1, :] = pos_ref[bead, component : component + 1, :]
            at = row_of(component, 1, bead)
            state[0, at : at + 1, :] = mom_ref[bead, component : component + 1, :] * inverse

    def ghost_rows_of(block, side):
        chunks = [block[:, m * LANES : (m + 1) * LANES] for m in range(atom_chunks)]
        parts = []
        for g in range(ghost_chunks):
            index = ghost_ref[1 - side : 2 - side, g * LANES : (g + 1) * LANES]
            index = jnp.broadcast_to(index, (TILE, LANES))
            parts.append(pick(chunks, index & (LANES - 1), index // LANES))
        return parts

    def send_ghosts(step, extra):
        for side in range(2):
            for tile in range(rows // TILE + 1):
                at = tile * TILE
                block = extra if tile == rows // TILE else state[step, at : at + TILE, :]
                if block is None:
                    block = jnp.zeros((TILE, atoms), jnp.float32)
                for g, part in enumerate(ghost_rows_of(block, side)):
                    ghost_out[step, side, at : at + TILE, g * LANES : (g + 1) * LANES] = part
        return [
            to_side(ghost_out.at[step, side], ghost_in.at[step, side],
                    ghost_s.at[step], ghost_r.at[step], side)
            for side in range(2)
        ]

    def spread_row(row):
        return jnp.broadcast_to(row, (TILE, LANES))

    def ghost_window(buffer, lead, row):
        def parts(side):
            return [
                spread_row(buffer[(*lead, side, slice(row, row + 1), slice(g * LANES, (g + 1) * LANES))])
                for g in range(ghost_chunks)
            ]
        return parts(0), parts(1)

    def window_of(step, row):
        low, high = ghost_window(ghost_in, (step,), row)
        own = [
            spread_row(state[step, row : row + 1, m * LANES : (m + 1) * LANES])
            for m in range(atom_chunks)
        ]
        return low + own + high

    def cheap(step):
        @pl.loop(0, atom_chunks)
        def _(j):
            lanes = pl.ds(pl.multiple_of(j * LANES, LANES), LANES)
            factor = whole[1, 0:1, lanes]
            indices = [near_ref[k : k + TILE, lanes] for k in range(0, slots, TILE)]
            lows = [index & (LANES - 1) for index in indices]
            highs = [index // LANES for index in indices]
            for bead in range(per_device):
                offsets = []
                for component in range(3):
                    row = row_of(component, 0, bead)
                    chunks = window_of(step, row)
                    middle = spread_row(state[step, row : row + 1, lanes])
                    offsets.append(
                        [pick(chunks, low, high) - middle for low, high in zip(lows, highs)]
                    )
                totals = [None] * 3
                for t in range(len(indices)):
                    squared = sum(offsets[c][t] * offsets[c][t] for c in range(3))
                    strength = weight[t * TILE : (t + 1) * TILE, lanes] * jnp.exp(
                        -squared / pair_width
                    )
                    for c in range(3):
                        term = strength * offsets[c][t]
                        totals[c] = term if totals[c] is None else totals[c] + term
                for c in range(3):
                    row = row_of(c, 1, bead)
                    total = jnp.sum(totals[c], axis=0, keepdims=True)
                    kick[row : row + 1, lanes] = pair_strength * factor * total

    def learned(low_high, slot):
        rates = radial_rates(w_in_ref.shape[1])
        for t in range(cover // LANES):
            lanes = pl.ds(pl.multiple_of(first + t * LANES, LANES), LANES)
            indices = [near_ref[k : k + TILE, lanes] for k in range(0, slots, TILE)]
            offsets = []
            for c in range(3):
                low, high = low_high(c)
                own = [
                    spread_row(whole[0, c : c + 1, m * LANES : (m + 1) * LANES])
                    for m in range(atom_chunks)
                ]
                chunks = low + own + high
                middle = spread_row(whole[0, c : c + 1, lanes])
                offsets.append(
                    [pick(chunks, index & (LANES - 1), index // LANES) - middle for index in indices]
                )
            bases = []
            messages = [None] * len(rates)
            for k in range(len(indices)):
                squared = sum(offsets[c][k] * offsets[c][k] for c in range(3))
                basis = [jnp.exp(-float(rates[r]) * squared) for r in range(2)]
                for r in range(2, len(rates)):
                    basis.append(basis[r - 2] * basis[r - 2])
                bases.append(basis)
                strength = weight[k * TILE : (k + 1) * TILE, lanes]
                for r in range(len(rates)):
                    term = strength * basis[r]
                    messages[r] = term if messages[r] is None else messages[r] + term
            message = jnp.concatenate(
                [jnp.sum(m, axis=0, keepdims=True) for m in messages], axis=0
            ) / slots
            hidden = dot(w_in_ref[...], message)
            hidden = hidden * jax.nn.sigmoid(hidden)
            radial = dot(w_out_ref[...], hidden)
            spread_radial = [spread_row(radial[r : r + 1, :]) for r in range(len(rates))]
            totals = [None] * 3
            for k in range(len(indices)):
                profile = sum(spread_radial[r] * bases[k][r] for r in range(len(rates)))
                strength = weight[k * TILE : (k + 1) * TILE, lanes] * profile
                for c in range(3):
                    term = strength * offsets[c][k]
                    totals[c] = term if totals[c] is None else totals[c] + term
            which = lax.broadcasted_iota(jnp.int32, (TILE, LANES), 0)
            tile = jnp.zeros((TILE, LANES), jnp.float32)
            for c in range(3):
                total = spread_row(jnp.sum(totals[c], axis=0, keepdims=True))
                tile = jnp.where(which == c, total, tile)
            piece[slot, me, :, t * LANES : (t + 1) * LANES] = tile

    def send_piece(slot):
        return [
            to_peer(piece.at[slot, me], piece.at[slot, me], piece_s.at[slot], piece_r.at[slot], j)
            for j in range(1, devices)
        ]

    def await_blocks(buffer, send, recv):
        for j in range(1, devices):
            to_peer(buffer.at[senders[j]], buffer.at[senders[j]], send, recv, j).wait_recv()

    def all_pieces(slot):
        parts = []
        for c in range(CB):
            line = []
            for m in range(atom_chunks):
                source = c * groups + m * LANES // share
                start = m * LANES - (source % groups) * share // LANES * LANES
                line.append(piece[slot, source, :, start : start + LANES])
            parts.append(jnp.concatenate(line, axis=1))
        return jnp.concatenate(parts, axis=0)

    sent = []

    def start(copies):
        for copy in copies:
            copy.start()
            sent.append(copy)

    parts = dot(share_ref[me], state[0])
    for c in range(CB):
        part_out[c] = parts[c * TILE : (c + 1) * TILE, :]
    copies = [
        to_peer(part_out.at[peers[j] // groups], part_in.at[me], part_s, part_r, j)
        for j in range(1, devices)
    ]
    ghost_copies = send_ghosts(0, jnp.broadcast_to(charge, (TILE, atoms)))
    whole[1] = jnp.broadcast_to(charge * inverse, (TILE, atoms))

    pl.semaphore_wait(barrier, devices + 1)
    start(copies)
    start(ghost_copies)
    await_blocks(part_in, part_s, part_r)
    contracted = part_out[member]
    for j in range(1, devices):
        contracted = contracted + part_in[senders[j]]
    whole[0] = contracted
    for side in range(2):
        for g, part in enumerate(ghost_rows_of(contracted, side)):
            qghost_out[side, :, g * LANES : (g + 1) * LANES] = part
    qcopies = [
        to_side(qghost_out.at[side], qghost_in.at[side], qghost_s, qghost_r, side)
        for side in range(2)
    ]
    start(qcopies)
    for copy in ghost_copies:
        copy.wait_recv()

    low, high = ghost_window(ghost_in, (0,), rows)
    own = [spread_row(charge[:, m * LANES : (m + 1) * LANES]) for m in range(atom_chunks)]
    chunks = low + own + high
    for m in range(atom_chunks):
        lanes = slice(m * LANES, (m + 1) * LANES)
        itself = ghosts + m * LANES + lax.broadcasted_iota(jnp.int32, (TILE, LANES), 1)
        for k in range(0, slots, TILE):
            index = near_ref[k : k + TILE, lanes]
            value = pick(chunks, index & (LANES - 1), index // LANES)
            weight[k : k + TILE, lanes] = jnp.where(index == itself, 0.0, value)

    cheap(0)
    gathered[0, me] = state[0] + (0.5 * inner_step) * kick[...]
    start([
        to_peer(gathered.at[0, me], gathered.at[0, me], all_s.at[0], all_r.at[0], j)
        for j in range(1, devices)
    ])
    for copy in qcopies:
        copy.wait_recv()
    learned(lambda c: ghost_window(qghost_in, (), c), 0)
    start(send_piece(0))
    await_blocks(gathered.at[0], all_s.at[0], all_r.at[0])
    await_blocks(piece.at[0], piece_s.at[0], piece_r.at[0])

    for step in range(1, NINNER + 1):
        every = gathered[step - 1].reshape(devices * rows, atoms)
        fresh = dot(move_ref[me], every)
        if step == 1:
            fresh = fresh + dot(mspread_ref[me], all_pieces(0) * inverse)
        state[step] = fresh
        extra = None
        if step == NINNER:
            extra = dot(moved_ref[member], every)
            whole[0] = extra
        ghost_copies = send_ghosts(step, extra)
        start(ghost_copies)
        for copy in ghost_copies:
            copy.wait_recv()
        if step == NINNER:
            learned(lambda c: ghost_window(ghost_in, (step,), rows + c), 1)
            start(send_piece(1))
        cheap(step)
        if step < NINNER:
            gathered[step, me] = state[step] + inner_step * kick[...]
            start([
                to_peer(gathered.at[step, me], gathered.at[step, me],
                        all_s.at[step], all_r.at[step], j)
                for j in range(1, devices)
            ])
            await_blocks(gathered.at[step], all_s.at[step], all_r.at[step])

    await_blocks(piece.at[1], piece_s.at[1], piece_r.at[1])
    kick[...] = (state[NINNER] + (0.5 * inner_step) * kick[...]) * mass + dot(
        spread_ref[me], all_pieces(1)
    )
    for component in range(3):
        for bead in range(per_device):
            at = row_of(component, 0, bead)
            new_pos_ref[bead, component : component + 1, :] = state[NINNER, at : at + 1, :]
            at = row_of(component, 1, bead)
            new_mom_ref[bead, component : component + 1, :] = kick[at : at + 1, :]
    for copy in sent:
        copy.wait_send()


def body(
    positions, momenta, neighbours, ghost_rows, species, species_scale, mass_table, w_in, w_out
):
    per_device, _, atoms = positions.shape
    slots = neighbours.shape[0]
    ghosts = ghost_rows.shape[0] // 2
    devices = lax.axis_size("bead")
    consts = tables(devices, per_device)
    rows = consts[0].shape[1]
    cover = max(atoms // (devices // CB), LANES)
    vmem = pl.BlockSpec(memory_space=pltpu.VMEM)
    smem = pl.BlockSpec(memory_space=pltpu.SMEM)
    f32 = jnp.float32
    dma = pltpu.SemaphoreType.DMA
    shape = jax.ShapeDtypeStruct(positions.shape, f32)
    return pl.pallas_call(
        cycle_kernel,
        name="cycle",
        out_shape=(shape, shape),
        in_specs=[vmem] * 5 + [smem] * 2 + [vmem] * 7,
        out_specs=(vmem, vmem),
        scratch_shapes=[
            pltpu.VMEM((NINNER + 1, rows, atoms), f32),
            pltpu.VMEM((rows, atoms), f32),
            pltpu.VMEM((slots, atoms), f32),
            pltpu.VMEM((NINNER, devices, rows, atoms), f32),
            pltpu.VMEM((NINNER + 1, 2, rows + TILE, ghosts), f32),
            pltpu.VMEM((NINNER + 1, 2, rows + TILE, ghosts), f32),
            pltpu.VMEM((CB, TILE, atoms), f32),
            pltpu.VMEM((devices, TILE, atoms), f32),
            pltpu.VMEM((2, TILE, atoms), f32),
            pltpu.VMEM((2, TILE, ghosts), f32),
            pltpu.VMEM((2, TILE, ghosts), f32),
            pltpu.VMEM((2, devices, TILE, cover), f32),
            dma((devices,)), dma((devices,)),
            dma((NINNER + 1, 2)), dma((NINNER + 1, 2)),
            dma((2,)), dma((2,)),
            dma((NINNER, devices)), dma((NINNER, devices)),
            dma((2, devices)), dma((2, devices)),
        ],
        compiler_params=pltpu.CompilerParams(
            collective_id=0, has_side_effects=True, vmem_limit_bytes=32 * 1024 * 1024
        ),
    )(
        positions, momenta, neighbours, ghost_rows.reshape(2, ghosts), species.reshape(1, atoms),
        species_scale, mass_table, w_in, w_out, *consts,
    )


def solution(mesh):
    in_specs = (
        P("bead", None, "space"),
        P("bead", None, "space"),
        P(None, "space"),
        P("space"),
        P("space"),
        P(),
        P(),
        P(),
        P(),
    )
    out_specs = (P("bead", None, "space"), P("bead", None, "space"))
    return jax.shard_map(body, mesh=mesh, in_specs=in_specs, out_specs=out_specs, check_vma=False)
```

```python
import jax
import jax.numpy as jnp
import numpy as np
from jax import lax
from jax.experimental import pallas as pl
from jax.experimental.pallas import tpu as pltpu
from jax.sharding import PartitionSpec as P

BEADS = 32
CB = 4
NINNER = 3


polymer_freq = 10.0
outer_step = 6.0
pair_width = 1.0
pair_strength = 1.0
highest = lax.Precision.HIGHEST


def mode_matrix(count):
    beadpos = np.arange(count)[None, :]
    modeidx = np.arange(count)[:, None]
    middle = count // 2
    cosine = np.sqrt(2.0 / count) * np.cos(2.0 * np.pi * beadpos * modeidx / count)
    sine_rows = np.sqrt(2.0 / count) * np.sin(2.0 * np.pi * beadpos * modeidx / count)
    matrix = np.where(modeidx < middle, cosine, sine_rows)
    matrix = np.where(modeidx == 0, 1.0 / np.sqrt(count), matrix)
    matrix = np.where(modeidx == middle, np.cos(np.pi * beadpos) / np.sqrt(count), matrix)
    return matrix


def mode_scales(count, inner_step):
    frequency = 2.0 * polymer_freq * np.sin(np.pi * np.arange(count) / count)
    nonzero = np.where(frequency > 0, frequency, 1.0)
    cosine = np.cos(frequency * inner_step)
    drift_gain = np.where(frequency > 0, np.sin(frequency * inner_step) / nonzero, inner_step)
    spring = frequency * np.sin(frequency * inner_step)
    return (cosine, drift_gain, spring)


def contraction(count, fewer):
    full_modes = mode_matrix(count)
    small_modes = mode_matrix(fewer)
    kept = list(range(fewer // 2 + 1)) + list(range(count - fewer // 2 + 1, count))
    contract = np.sqrt(fewer / count) * (small_modes.T @ full_modes[kept])
    expand = count / fewer * contract.T
    return (contract, expand)


def radial_rates(count):
    return 0.2 * 2.0 ** (np.arange(count) / 2.0)

LANES = 128
TILE = 8
MESH = pl.DeviceIdType.MESH


def tables(devices, per_device):
    inner_step = outer_step / NINNER
    modes = mode_matrix(BEADS)
    cosine, drift_gain, spring = mode_scales(BEADS, inner_step)
    persist = modes.T @ (cosine[:, None] * modes)
    coupling = modes.T @ (drift_gain[:, None] * modes)
    restoring = -(modes.T @ (spring[:, None] * modes))
    contract, expand = contraction(BEADS, CB)
    rows = -(-6 * per_device // TILE) * TILE
    full = devices * rows
    blocks = ((persist, coupling), (restoring, persist))

    def places(component, kind):
        bead = np.arange(BEADS)
        local = component * 2 * per_device + kind * per_device + bead % per_device
        return bead // per_device * rows + local

    move = np.zeros((full, full))
    reduce = np.zeros((CB, TILE, full))
    spread = np.zeros((full, CB * TILE))
    for component in range(3):
        for out in range(2):
            for kind in range(2):
                move[np.ix_(places(component, out), places(component, kind))] = blocks[out][kind]
        for member in range(CB):
            reduce[member, component, places(component, 0)] = contract[member]
            spread[places(component, 1), member * TILE + component] = (
                0.5 * outer_step * expand[:, member]
            )
    reduce_moved = np.repeat(reduce @ move, devices // CB, axis=0)
    move_spread = (move @ spread).reshape(devices, rows, CB * TILE)
    share = reduce.reshape(CB * TILE, devices, rows).transpose(1, 0, 2)
    spread = spread.reshape(devices, rows, CB * TILE)
    move = np.concatenate((move.reshape(devices, rows, full), move_spread), axis=2)

    def padded(table):
        return np.pad(table, ((0, 0), (0, 0), (0, move.shape[2] - table.shape[2])))

    stacked = (move, padded(reduce_moved), padded(spread), padded(share))
    return jnp.asarray(np.concatenate(stacked, axis=1), jnp.float32)


def dot(a, b):
    return jnp.dot(a, b, precision=highest, preferred_element_type=jnp.float32)


def pick(chunks, low, high):
    found = None
    for number, chunk in enumerate(chunks):
        value = jnp.take_along_axis(chunk, low, axis=1, mode="promise_in_bounds")
        found = value if found is None else jnp.where(high == number, value, found)
    return found


def cycle_kernel(
    pos_in, mom_in, near_in, ghost_from, species_in, scale_in, mass_in, w_in_in, w_out_in, table_in,
    new_pos_ref, new_mom_ref,
    state, kick, weight, gathered, ghost_out, ghost_in, part_out, part_in, whole,
    qghost_out, qghost_in, piece,
    pos_ref, mom_ref, near_ref, ghost_ref, species_ref, scale_ref, mass_ref, w_in_ref, w_out_ref,
    table_ref, load_s,
    part_s, part_r, ghost_s, ghost_r, qghost_s, qghost_r, all_s, all_r, piece_s, piece_r,
):
    _, per_device, atoms = pos_ref.shape
    slots = near_ref.shape[0]
    rows = state.shape[1]
    ghosts = ghost_ref.shape[1]
    devices = lax.axis_size("bead")
    domains = lax.axis_size("space")
    me = lax.axis_index("bead")
    domain = lax.axis_index("space")
    above = lax.rem(domain + 1, domains)
    below = lax.rem(domain + domains - 1, domains)
    peers = [lax.rem(me + j, devices) for j in range(devices)]
    senders = [lax.rem(me + devices - j, devices) for j in range(devices)]
    inner_step = outer_step / NINNER
    groups = devices // CB
    share = atoms // groups
    cover = piece.shape[3]
    member = me // groups
    first = lax.rem(me, groups) * share // LANES * LANES
    ghost_chunks = ghosts // LANES
    atom_chunks = atoms // LANES

    loads = [
        pltpu.make_async_copy(src, dst, load_s.at[number])
        for number, (src, dst) in enumerate((
            (pos_in, pos_ref), (mom_in, mom_ref), (species_in, species_ref), (scale_in, scale_ref),
            (mass_in, mass_ref), (table_in.at[me], table_ref), (ghost_from, ghost_ref),
            (near_in, near_ref), (w_in_in, w_in_ref), (w_out_in, w_out_ref),
        ))
    ]
    for load in loads:
        load.start()
    barrier = pltpu.get_barrier_semaphore()
    for j in range(1, devices):
        pl.semaphore_signal(barrier, inc=1, device_id={"bead": peers[j]}, device_id_type=MESH)
    for target in (above, below):
        pl.semaphore_signal(barrier, inc=1, device_id={"space": target}, device_id_type=MESH)

    def to_peer(src, dst, send, recv, j):
        return pltpu.make_async_remote_copy(
            src_ref=src, dst_ref=dst, send_sem=send.at[j], recv_sem=recv.at[j],
            device_id={"bead": peers[j]}, device_id_type=MESH,
        )

    def to_side(src, dst, send, recv, side):
        return pltpu.make_async_remote_copy(
            src_ref=src, dst_ref=dst, send_sem=send.at[side], recv_sem=recv.at[side],
            device_id={"space": (above, below)[side]}, device_id_type=MESH,
        )

    def row_of(component, kind, bead):
        return (component * 2 + kind) * per_device + bead

    full = devices * rows
    moved_row = rows
    spread_row_at = moved_row + TILE
    share_row = spread_row_at + rows
    for load in loads:
        load.wait()
    species = species_ref[...]
    charge = jnp.zeros((1, atoms), jnp.float32)
    mass = jnp.zeros((1, atoms), jnp.float32)
    for kind in range(scale_ref.shape[1]):
        charge = jnp.where(species == kind, scale_ref[0:1, kind : kind + 1], charge)
        mass = jnp.where(species == kind, mass_ref[0:1, kind : kind + 1], mass)
    inverse = 1.0 / mass

    kick[...] = jnp.zeros(kick.shape, jnp.float32)
    if rows > 6 * per_device:
        state[0] = jnp.zeros((rows, atoms), jnp.float32)
    for component in range(3):
        at = row_of(component, 0, 0)
        state[0, at : at + per_device, :] = pos_ref[component]
        at = row_of(component, 1, 0)
        state[0, at : at + per_device, :] = mom_ref[component] * inverse

    def ghost_rows_of(block, side):
        chunks = [block[:, m * LANES : (m + 1) * LANES] for m in range(atom_chunks)]
        parts = []
        for g in range(ghost_chunks):
            index = ghost_ref[1 - side : 2 - side, g * LANES : (g + 1) * LANES]
            index = jnp.broadcast_to(index, (TILE, LANES))
            parts.append(pick(chunks, index & (LANES - 1), index // LANES))
        return parts

    def send_ghosts(step, extra):
        for side in range(2):
            for tile in range(rows // TILE + 1):
                at = tile * TILE
                block = extra if tile == rows // TILE else state[step, at : at + TILE, :]
                if block is None:
                    block = jnp.zeros((TILE, atoms), jnp.float32)
                for g, part in enumerate(ghost_rows_of(block, side)):
                    ghost_out[step, side, at : at + TILE, g * LANES : (g + 1) * LANES] = part
        return [
            to_side(ghost_out.at[step, side], ghost_in.at[step, side],
                    ghost_s.at[step], ghost_r.at[step], side)
            for side in range(2)
        ]

    def spread_row(row):
        return jnp.broadcast_to(row, (TILE, LANES))

    def ghost_window(buffer, lead, row):
        def parts(side):
            return [
                spread_row(buffer[(*lead, side, slice(row, row + 1), slice(g * LANES, (g + 1) * LANES))])
                for g in range(ghost_chunks)
            ]
        return parts(0), parts(1)

    def window_of(step, row):
        low, high = ghost_window(ghost_in, (step,), row)
        own = [
            spread_row(state[step, row : row + 1, m * LANES : (m + 1) * LANES])
            for m in range(atom_chunks)
        ]
        return low + own + high

    def cheap(step):
        @pl.loop(0, atom_chunks)
        def _(j):
            lanes = pl.ds(pl.multiple_of(j * LANES, LANES), LANES)
            factor = whole[1, 0:1, lanes]
            indices = [near_ref[k : k + TILE, lanes] for k in range(0, slots, TILE)]
            lows = [index & (LANES - 1) for index in indices]
            highs = [index // LANES for index in indices]
            for bead in range(per_device):
                offsets = []
                for component in range(3):
                    row = row_of(component, 0, bead)
                    chunks = window_of(step, row)
                    middle = spread_row(state[step, row : row + 1, lanes])
                    offsets.append(
                        [pick(chunks, low, high) - middle for low, high in zip(lows, highs)]
                    )
                totals = [None] * 3
                for t in range(len(indices)):
                    squared = sum(offsets[c][t] * offsets[c][t] for c in range(3))
                    strength = weight[t * TILE : (t + 1) * TILE, lanes] * jnp.exp(
                        -squared / pair_width
                    )
                    for c in range(3):
                        term = strength * offsets[c][t]
                        totals[c] = term if totals[c] is None else totals[c] + term
                for c in range(3):
                    row = row_of(c, 1, bead)
                    total = jnp.sum(totals[c], axis=0, keepdims=True)
                    kick[row : row + 1, lanes] = pair_strength * factor * total

    def learned(low_high, slot):
        rates = radial_rates(w_in_ref.shape[0])
        for t in range(cover // LANES):
            lanes = pl.ds(pl.multiple_of(first + t * LANES, LANES), LANES)
            indices = [near_ref[k : k + TILE, lanes] for k in range(0, slots, TILE)]
            offsets = []
            for c in range(3):
                low, high = low_high(c)
                own = [
                    spread_row(whole[0, c : c + 1, m * LANES : (m + 1) * LANES])
                    for m in range(atom_chunks)
                ]
                chunks = low + own + high
                middle = spread_row(whole[0, c : c + 1, lanes])
                offsets.append(
                    [pick(chunks, index & (LANES - 1), index // LANES) - middle for index in indices]
                )
            bases = []
            messages = [None] * len(rates)
            for k in range(len(indices)):
                squared = sum(offsets[c][k] * offsets[c][k] for c in range(3))
                basis = [jnp.exp(-float(rates[r]) * squared) for r in range(2)]
                for r in range(2, len(rates)):
                    basis.append(basis[r - 2] * basis[r - 2])
                bases.append(basis)
                strength = weight[k * TILE : (k + 1) * TILE, lanes]
                for r in range(len(rates)):
                    term = strength * basis[r]
                    messages[r] = term if messages[r] is None else messages[r] + term
            message = jnp.concatenate(
                [jnp.sum(m, axis=0, keepdims=True) for m in messages], axis=0
            ) / slots
            hidden = lax.dot_general(
                w_in_ref[...], message, (((0,), (0,)), ((), ())),
                precision=highest, preferred_element_type=jnp.float32,
            )
            hidden = hidden * jax.nn.sigmoid(hidden)
            radial = dot(w_out_ref[...], hidden)
            spread_radial = [spread_row(radial[r : r + 1, :]) for r in range(len(rates))]
            totals = [None] * 3
            for k in range(len(indices)):
                profile = sum(spread_radial[r] * bases[k][r] for r in range(len(rates)))
                strength = weight[k * TILE : (k + 1) * TILE, lanes] * profile
                for c in range(3):
                    term = strength * offsets[c][k]
                    totals[c] = term if totals[c] is None else totals[c] + term
            which = lax.broadcasted_iota(jnp.int32, (TILE, LANES), 0)
            tile = jnp.zeros((TILE, LANES), jnp.float32)
            for c in range(3):
                total = spread_row(jnp.sum(totals[c], axis=0, keepdims=True))
                tile = jnp.where(which == c, total, tile)
            piece[slot, me, :, t * LANES : (t + 1) * LANES] = tile

    def send_piece(slot):
        return [
            to_peer(piece.at[slot, me], piece.at[slot, me], piece_s.at[slot], piece_r.at[slot], j)
            for j in range(1, devices)
        ]

    def await_blocks(buffer, send, recv):
        for j in range(1, devices):
            to_peer(buffer.at[senders[j]], buffer.at[senders[j]], send, recv, j).wait_recv()

    def all_pieces(slot):
        parts = []
        for c in range(CB):
            line = []
            for m in range(atom_chunks):
                source = c * groups + m * LANES // share
                start = m * LANES - (source % groups) * share // LANES * LANES
                line.append(piece[slot, source, :, start : start + LANES])
            parts.append(jnp.concatenate(line, axis=1))
        return jnp.concatenate(parts, axis=0)

    sent = []

    def start(copies):
        for copy in copies:
            copy.start()
            sent.append(copy)

    parts = dot(table_ref[share_row : share_row + CB * TILE, 0:rows], state[0])
    for c in range(CB):
        part_out[c] = parts[c * TILE : (c + 1) * TILE, :]
    copies = [
        to_peer(part_out.at[peers[j] // groups], part_in.at[me], part_s, part_r, j)
        for j in range(1, devices)
    ]
    ghost_copies = send_ghosts(0, jnp.broadcast_to(charge, (TILE, atoms)))
    whole[1] = jnp.broadcast_to(charge * inverse, (TILE, atoms))

    pl.semaphore_wait(barrier, devices + 1)
    start(copies)
    start(ghost_copies)
    await_blocks(part_in, part_s, part_r)
    contracted = part_out[member]
    for j in range(1, devices):
        contracted = contracted + part_in[senders[j]]
    whole[0] = contracted
    for side in range(2):
        for g, part in enumerate(ghost_rows_of(contracted, side)):
            qghost_out[side, :, g * LANES : (g + 1) * LANES] = part
    qcopies = [
        to_side(qghost_out.at[side], qghost_in.at[side], qghost_s, qghost_r, side)
        for side in range(2)
    ]
    start(qcopies)
    for copy in ghost_copies:
        copy.wait_recv()

    low, high = ghost_window(ghost_in, (0,), rows)
    own = [spread_row(charge[:, m * LANES : (m + 1) * LANES]) for m in range(atom_chunks)]
    chunks = low + own + high
    for m in range(atom_chunks):
        lanes = slice(m * LANES, (m + 1) * LANES)
        itself = ghosts + m * LANES + lax.broadcasted_iota(jnp.int32, (TILE, LANES), 1)
        for k in range(0, slots, TILE):
            index = near_ref[k : k + TILE, lanes]
            value = pick(chunks, index & (LANES - 1), index // LANES)
            weight[k : k + TILE, lanes] = jnp.where(index == itself, 0.0, value)

    cheap(0)
    gathered[0, me] = state[0] + (0.5 * inner_step) * kick[...]
    start([
        to_peer(gathered.at[0, me], gathered.at[0, me], all_s.at[0], all_r.at[0], j)
        for j in range(1, devices)
    ])
    for copy in qcopies:
        copy.wait_recv()
    learned(lambda c: ghost_window(qghost_in, (), c), 0)
    start(send_piece(0))
    await_blocks(gathered.at[0], all_s.at[0], all_r.at[0])
    await_blocks(piece.at[0], piece_s.at[0], piece_r.at[0])

    for step in range(1, NINNER + 1):
        every = gathered[step - 1].reshape(devices * rows, atoms)
        extra = None
        if step == 1:
            every = jnp.concatenate((every, all_pieces(0) * inverse), axis=0)
            fresh = dot(table_ref[0:rows, :], every)
        elif step < NINNER:
            fresh = dot(table_ref[0:rows, 0:full], every)
        else:
            both = dot(table_ref[0 : moved_row + TILE, 0:full], every)
            fresh = both[0:rows]
            extra = both[moved_row:]
            whole[0] = extra
        state[step] = fresh
        ghost_copies = send_ghosts(step, extra)
        start(ghost_copies)
        for copy in ghost_copies:
            copy.wait_recv()
        if step == NINNER:
            learned(lambda c: ghost_window(ghost_in, (step,), rows + c), 1)
            start(send_piece(1))
        cheap(step)
        if step < NINNER:
            gathered[step, me] = state[step] + inner_step * kick[...]
            start([
                to_peer(gathered.at[step, me], gathered.at[step, me],
                        all_s.at[step], all_r.at[step], j)
                for j in range(1, devices)
            ])
            await_blocks(gathered.at[step], all_s.at[step], all_r.at[step])

    await_blocks(piece.at[1], piece_s.at[1], piece_r.at[1])
    kick[...] = (state[NINNER] + (0.5 * inner_step) * kick[...]) * mass + dot(
        table_ref[spread_row_at : spread_row_at + rows, 0 : CB * TILE], all_pieces(1)
    )
    for component in range(3):
        at = row_of(component, 0, 0)
        new_pos_ref[component] = state[NINNER, at : at + per_device, :]
        at = row_of(component, 1, 0)
        new_mom_ref[component] = kick[at : at + per_device, :]
    for copy in sent:
        copy.wait_send()


def body(
    positions, momenta, neighbours, ghost_rows, species, species_scale, mass_table, w_in, w_out
):
    per_device, _, atoms = positions.shape
    slots = neighbours.shape[0]
    ghosts = ghost_rows.shape[0] // 2
    devices = lax.axis_size("bead")
    table = tables(devices, per_device)
    rows = -(-6 * per_device // TILE) * TILE
    cover = max(atoms // (devices // CB), LANES)
    vmem = pl.BlockSpec(memory_space=pltpu.VMEM)
    hbm = pl.BlockSpec(memory_space=pltpu.HBM)
    f32 = jnp.float32
    dma = pltpu.SemaphoreType.DMA
    operands = (
        positions.transpose(1, 0, 2), momenta.transpose(1, 0, 2), neighbours,
        ghost_rows.reshape(2, ghosts), species.reshape(1, atoms), species_scale.reshape(1, -1),
        mass_table.reshape(1, -1), w_in.T, w_out, table,
    )
    shape = jax.ShapeDtypeStruct(operands[0].shape, f32)
    new_positions, new_momenta = pl.pallas_call(
        cycle_kernel,
        name="cycle",
        out_shape=(shape, shape),
        in_specs=[hbm] * 10,
        out_specs=(vmem, vmem),
        scratch_shapes=[
            pltpu.VMEM((NINNER + 1, rows, atoms), f32),
            pltpu.VMEM((rows, atoms), f32),
            pltpu.VMEM((slots, atoms), f32),
            pltpu.VMEM((NINNER, devices, rows, atoms), f32),
            pltpu.VMEM((NINNER + 1, 2, rows + TILE, ghosts), f32),
            pltpu.VMEM((NINNER + 1, 2, rows + TILE, ghosts), f32),
            pltpu.VMEM((CB, TILE, atoms), f32),
            pltpu.VMEM((devices, TILE, atoms), f32),
            pltpu.VMEM((2, TILE, atoms), f32),
            pltpu.VMEM((2, TILE, ghosts), f32),
            pltpu.VMEM((2, TILE, ghosts), f32),
            pltpu.VMEM((2, devices, TILE, cover), f32),
            *[pltpu.VMEM(operand.shape, operand.dtype) for operand in operands[:-1]],
            pltpu.VMEM(table.shape[1:], f32),
            dma((len(operands),)),
            dma((devices,)), dma((devices,)),
            dma((NINNER + 1, 2)), dma((NINNER + 1, 2)),
            dma((2,)), dma((2,)),
            dma((NINNER, devices)), dma((NINNER, devices)),
            dma((2, devices)), dma((2, devices)),
        ],
        compiler_params=pltpu.CompilerParams(
            collective_id=0, has_side_effects=True, vmem_limit_bytes=67043328
        ),
    )(*operands)
    return (new_positions.transpose(1, 0, 2), new_momenta.transpose(1, 0, 2))


def solution(mesh):
    in_specs = (
        P("bead", None, "space"),
        P("bead", None, "space"),
        P(None, "space"),
        P("space"),
        P("space"),
        P(),
        P(),
        P(),
        P(),
    )
    out_specs = (P("bead", None, "space"), P("bead", None, "space"))
    return jax.shard_map(body, mesh=mesh, in_specs=in_specs, out_specs=out_specs, check_vma=False)
```

```python
import jax
import jax.numpy as jnp
import numpy as np
from jax import lax
from jax.experimental import pallas as pl
from jax.experimental.pallas import tpu as pltpu
from jax.sharding import PartitionSpec as P

BEADS = 32
CB = 4
NINNER = 3


polymer_freq = 10.0
outer_step = 6.0
pair_width = 1.0
pair_strength = 1.0
highest = lax.Precision.HIGHEST


def mode_matrix(count):
    beadpos = np.arange(count)[None, :]
    modeidx = np.arange(count)[:, None]
    middle = count // 2
    cosine = np.sqrt(2.0 / count) * np.cos(2.0 * np.pi * beadpos * modeidx / count)
    sine_rows = np.sqrt(2.0 / count) * np.sin(2.0 * np.pi * beadpos * modeidx / count)
    matrix = np.where(modeidx < middle, cosine, sine_rows)
    matrix = np.where(modeidx == 0, 1.0 / np.sqrt(count), matrix)
    matrix = np.where(modeidx == middle, np.cos(np.pi * beadpos) / np.sqrt(count), matrix)
    return matrix


def mode_scales(count, inner_step):
    frequency = 2.0 * polymer_freq * np.sin(np.pi * np.arange(count) / count)
    nonzero = np.where(frequency > 0, frequency, 1.0)
    cosine = np.cos(frequency * inner_step)
    drift_gain = np.where(frequency > 0, np.sin(frequency * inner_step) / nonzero, inner_step)
    spring = frequency * np.sin(frequency * inner_step)
    return (cosine, drift_gain, spring)


def contraction(count, fewer):
    full_modes = mode_matrix(count)
    small_modes = mode_matrix(fewer)
    kept = list(range(fewer // 2 + 1)) + list(range(count - fewer // 2 + 1, count))
    contract = np.sqrt(fewer / count) * (small_modes.T @ full_modes[kept])
    expand = count / fewer * contract.T
    return (contract, expand)


def radial_rates(count):
    return 0.2 * 2.0 ** (np.arange(count) / 2.0)

LANES = 128
TILE = 8
MESH = pl.DeviceIdType.MESH


def tables(devices, per_device):
    inner_step = outer_step / NINNER
    modes = mode_matrix(BEADS)
    cosine, drift_gain, spring = mode_scales(BEADS, inner_step)
    persist = modes.T @ (cosine[:, None] * modes)
    coupling = modes.T @ (drift_gain[:, None] * modes)
    restoring = -(modes.T @ (spring[:, None] * modes))
    contract, expand = contraction(BEADS, CB)
    rows = -(-6 * per_device // TILE) * TILE
    full = devices * rows
    blocks = ((persist, coupling), (restoring, persist))

    def places(component, kind):
        bead = np.arange(BEADS)
        local = component * 2 * per_device + kind * per_device + bead % per_device
        return bead // per_device * rows + local

    move = np.zeros((full, full))
    reduce = np.zeros((CB, TILE, full))
    spread = np.zeros((full, CB * TILE))
    for component in range(3):
        for out in range(2):
            for kind in range(2):
                move[np.ix_(places(component, out), places(component, kind))] = blocks[out][kind]
        for member in range(CB):
            reduce[member, component, places(component, 0)] = contract[member]
            spread[places(component, 1), member * TILE + component] = (
                0.5 * outer_step * expand[:, member]
            )
    reduce_moved = np.repeat(reduce @ move, devices // CB, axis=0)
    move_spread = (move @ spread).reshape(devices, rows, CB * TILE)
    share = reduce.reshape(CB * TILE, devices, rows).transpose(1, 0, 2)
    spread = spread.reshape(devices, rows, CB * TILE)
    move = np.concatenate((move.reshape(devices, rows, full), move_spread), axis=2)

    def padded(table):
        return np.pad(table, ((0, 0), (0, 0), (0, move.shape[2] - table.shape[2])))

    stacked = (move, padded(reduce_moved), padded(spread), padded(share))
    return jnp.asarray(np.concatenate(stacked, axis=1), jnp.float32)


def dot(a, b):
    return jnp.dot(a, b, precision=highest, preferred_element_type=jnp.float32)


def pick(chunks, low, high):
    found = None
    for number, chunk in enumerate(chunks):
        value = jnp.take_along_axis(chunk, low, axis=1, mode="promise_in_bounds")
        found = value if found is None else jnp.where(high == number, value, found)
    return found


def cycle_kernel(
    pos_in, mom_in, near_in, ghost_from, species_in, scale_in, mass_in, w_in_in, w_out_in, table_in,
    new_pos_ref, new_mom_ref,
    state, kick, weight, gathered, ghost_out, ghost_in, part_out, part_in, whole,
    qghost_out, qghost_in, piece, edge_out, edge_in,
    pos_ref, mom_ref, near_ref, ghost_ref, species_ref, scale_ref, mass_ref, w_in_ref, w_out_ref,
    table_ref, load_s, edge_s, edge_r,
    part_s, part_r, ghost_s, ghost_r, qghost_s, qghost_r, all_s, all_r, piece_s, piece_r,
):
    _, per_device, atoms = pos_ref.shape
    slots = near_ref.shape[0]
    rows = state.shape[1]
    ghosts = ghost_ref.shape[1]
    devices = lax.axis_size("bead")
    domains = lax.axis_size("space")
    me = lax.axis_index("bead")
    domain = lax.axis_index("space")
    above = lax.rem(domain + 1, domains)
    below = lax.rem(domain + domains - 1, domains)
    peers = [lax.rem(me + j, devices) for j in range(devices)]
    senders = [lax.rem(me + devices - j, devices) for j in range(devices)]
    inner_step = outer_step / NINNER
    groups = devices // CB
    share = atoms // groups
    cover = piece.shape[3]
    member = me // groups
    first = lax.rem(me, groups) * share // LANES * LANES
    ghost_chunks = ghosts // LANES
    atom_chunks = atoms // LANES

    loads = [
        pltpu.make_async_copy(src, dst, load_s.at[number])
        for number, (src, dst) in enumerate((
            (pos_in, pos_ref), (mom_in, mom_ref), (species_in, species_ref), (scale_in, scale_ref),
            (mass_in, mass_ref), (table_in.at[me], table_ref), (ghost_from, ghost_ref),
            (near_in, near_ref), (w_in_in, w_in_ref), (w_out_in, w_out_ref),
        ))
    ]
    for load in loads:
        load.start()
    barrier = pltpu.get_barrier_semaphore()
    for j in range(1, devices):
        pl.semaphore_signal(barrier, inc=1, device_id={"bead": peers[j]}, device_id_type=MESH)
    for target in (above, below):
        for j in range(devices):
            pl.semaphore_signal(
                barrier, inc=1, device_id={"bead": peers[j], "space": target}, device_id_type=MESH
            )

    def to_peer(src, dst, send, recv, j):
        return pltpu.make_async_remote_copy(
            src_ref=src, dst_ref=dst, send_sem=send.at[j], recv_sem=recv.at[j],
            device_id={"bead": peers[j]}, device_id_type=MESH,
        )

    def to_side(src, dst, send, recv, side):
        return pltpu.make_async_remote_copy(
            src_ref=src, dst_ref=dst, send_sem=send.at[side], recv_sem=recv.at[side],
            device_id={"space": (above, below)[side]}, device_id_type=MESH,
        )

    def to_edge(step, side, j):
        return pltpu.make_async_remote_copy(
            src_ref=edge_out.at[step, side], dst_ref=edge_in.at[step, side, me],
            send_sem=edge_s.at[step, side, j], recv_sem=edge_r.at[step, side, j],
            device_id={"bead": peers[j], "space": (above, below)[side]}, device_id_type=MESH,
        )

    def await_edges(step):
        for side in range(2):
            for j in range(devices):
                pltpu.make_async_remote_copy(
                    src_ref=edge_out.at[step, side], dst_ref=edge_in.at[step, side, senders[j]],
                    send_sem=edge_s.at[step, side, j], recv_sem=edge_r.at[step, side, j],
                    device_id={"bead": peers[j], "space": (above, below)[side]},
                    device_id_type=MESH,
                ).wait_recv()

    def row_of(component, kind, bead):
        return (component * 2 + kind) * per_device + bead

    full = devices * rows
    moved_row = rows
    spread_row_at = moved_row + TILE
    share_row = spread_row_at + rows
    for load in loads:
        load.wait()
    species = species_ref[...]
    charge = jnp.zeros((1, atoms), jnp.float32)
    mass = jnp.zeros((1, atoms), jnp.float32)
    for kind in range(scale_ref.shape[1]):
        charge = jnp.where(species == kind, scale_ref[0:1, kind : kind + 1], charge)
        mass = jnp.where(species == kind, mass_ref[0:1, kind : kind + 1], mass)
    inverse = 1.0 / mass

    kick[...] = jnp.zeros(kick.shape, jnp.float32)
    if rows > 6 * per_device:
        state[0] = jnp.zeros((rows, atoms), jnp.float32)
    for component in range(3):
        at = row_of(component, 0, 0)
        state[0, at : at + per_device, :] = pos_ref[component]
        at = row_of(component, 1, 0)
        state[0, at : at + per_device, :] = mom_ref[component] * inverse

    def ghost_rows_of(block, side):
        chunks = [block[:, m * LANES : (m + 1) * LANES] for m in range(atom_chunks)]
        parts = []
        for g in range(ghost_chunks):
            index = ghost_ref[1 - side : 2 - side, g * LANES : (g + 1) * LANES]
            index = jnp.broadcast_to(index, (TILE, LANES))
            parts.append(pick(chunks, index & (LANES - 1), index // LANES))
        return parts

    def send_ghosts(step, extra):
        for side in range(2):
            for tile in range(rows // TILE + 1):
                at = tile * TILE
                block = extra if tile == rows // TILE else state[step, at : at + TILE, :]
                if block is None:
                    block = jnp.zeros((TILE, atoms), jnp.float32)
                for g, part in enumerate(ghost_rows_of(block, side)):
                    ghost_out[step, side, at : at + TILE, g * LANES : (g + 1) * LANES] = part
        return [
            to_side(ghost_out.at[step, side], ghost_in.at[step, side],
                    ghost_s.at[step], ghost_r.at[step], side)
            for side in range(2)
        ]

    def spread_row(row):
        return jnp.broadcast_to(row, (TILE, LANES))

    def ghost_window(buffer, lead, row):
        def parts(side):
            return [
                spread_row(buffer[(*lead, side, slice(row, row + 1), slice(g * LANES, (g + 1) * LANES))])
                for g in range(ghost_chunks)
            ]
        return parts(0), parts(1)

    def window_of(step, row):
        low, high = ghost_window(ghost_in, (step,), row)
        own = [
            spread_row(state[step, row : row + 1, m * LANES : (m + 1) * LANES])
            for m in range(atom_chunks)
        ]
        return low + own + high

    def cheap(step):
        @pl.loop(0, atom_chunks)
        def _(j):
            lanes = pl.ds(pl.multiple_of(j * LANES, LANES), LANES)
            factor = whole[1, 0:1, lanes]
            indices = [near_ref[k : k + TILE, lanes] for k in range(0, slots, TILE)]
            lows = [index & (LANES - 1) for index in indices]
            highs = [index // LANES for index in indices]
            for bead in range(per_device):
                offsets = []
                for component in range(3):
                    row = row_of(component, 0, bead)
                    chunks = window_of(step, row)
                    middle = spread_row(state[step, row : row + 1, lanes])
                    offsets.append(
                        [pick(chunks, low, high) - middle for low, high in zip(lows, highs)]
                    )
                totals = [None] * 3
                for t in range(len(indices)):
                    squared = sum(offsets[c][t] * offsets[c][t] for c in range(3))
                    strength = weight[t * TILE : (t + 1) * TILE, lanes] * jnp.exp(
                        -squared / pair_width
                    )
                    for c in range(3):
                        term = strength * offsets[c][t]
                        totals[c] = term if totals[c] is None else totals[c] + term
                for c in range(3):
                    row = row_of(c, 1, bead)
                    total = jnp.sum(totals[c], axis=0, keepdims=True)
                    kick[row : row + 1, lanes] = pair_strength * factor * total

    def learned(low_high, slot):
        rates = radial_rates(w_in_ref.shape[0])
        for t in range(cover // LANES):
            lanes = pl.ds(pl.multiple_of(first + t * LANES, LANES), LANES)
            indices = [near_ref[k : k + TILE, lanes] for k in range(0, slots, TILE)]
            offsets = []
            for c in range(3):
                low, high = low_high(c)
                own = [
                    spread_row(whole[0, c : c + 1, m * LANES : (m + 1) * LANES])
                    for m in range(atom_chunks)
                ]
                chunks = low + own + high
                middle = spread_row(whole[0, c : c + 1, lanes])
                offsets.append(
                    [pick(chunks, index & (LANES - 1), index // LANES) - middle for index in indices]
                )
            bases = []
            messages = [None] * len(rates)
            for k in range(len(indices)):
                squared = sum(offsets[c][k] * offsets[c][k] for c in range(3))
                basis = [jnp.exp(-float(rates[r]) * squared) for r in range(2)]
                for r in range(2, len(rates)):
                    basis.append(basis[r - 2] * basis[r - 2])
                bases.append(basis)
                strength = weight[k * TILE : (k + 1) * TILE, lanes]
                for r in range(len(rates)):
                    term = strength * basis[r]
                    messages[r] = term if messages[r] is None else messages[r] + term
            message = jnp.concatenate(
                [jnp.sum(m, axis=0, keepdims=True) for m in messages], axis=0
            ) / slots
            hidden = lax.dot_general(
                w_in_ref[...], message, (((0,), (0,)), ((), ())),
                precision=highest, preferred_element_type=jnp.float32,
            )
            hidden = hidden * jax.nn.sigmoid(hidden)
            radial = dot(w_out_ref[...], hidden)
            spread_radial = [spread_row(radial[r : r + 1, :]) for r in range(len(rates))]
            totals = [None] * 3
            for k in range(len(indices)):
                profile = sum(spread_radial[r] * bases[k][r] for r in range(len(rates)))
                strength = weight[k * TILE : (k + 1) * TILE, lanes] * profile
                for c in range(3):
                    term = strength * offsets[c][k]
                    totals[c] = term if totals[c] is None else totals[c] + term
            which = lax.broadcasted_iota(jnp.int32, (TILE, LANES), 0)
            tile = jnp.zeros((TILE, LANES), jnp.float32)
            for c in range(3):
                total = spread_row(jnp.sum(totals[c], axis=0, keepdims=True))
                tile = jnp.where(which == c, total, tile)
            piece[slot, me, :, t * LANES : (t + 1) * LANES] = tile

    def send_piece(slot):
        return [
            to_peer(piece.at[slot, me], piece.at[slot, me], piece_s.at[slot], piece_r.at[slot], j)
            for j in range(1, devices)
        ]

    def await_blocks(buffer, send, recv):
        for j in range(1, devices):
            to_peer(buffer.at[senders[j]], buffer.at[senders[j]], send, recv, j).wait_recv()

    def all_pieces(slot):
        parts = []
        for c in range(CB):
            line = []
            for m in range(atom_chunks):
                source = c * groups + m * LANES // share
                start = m * LANES - (source % groups) * share // LANES * LANES
                line.append(piece[slot, source, :, start : start + LANES])
            parts.append(jnp.concatenate(line, axis=1))
        return jnp.concatenate(parts, axis=0)

    sent = []

    def start(copies):
        for copy in copies:
            copy.start()
            sent.append(copy)

    parts = dot(table_ref[share_row : share_row + CB * TILE, 0:rows], state[0])
    for c in range(CB):
        part_out[c] = parts[c * TILE : (c + 1) * TILE, :]
    copies = [
        to_peer(part_out.at[peers[j] // groups], part_in.at[me], part_s, part_r, j)
        for j in range(1, devices)
    ]
    ghost_copies = send_ghosts(0, jnp.broadcast_to(charge, (TILE, atoms)))
    whole[1] = jnp.broadcast_to(charge * inverse, (TILE, atoms))

    pl.semaphore_wait(barrier, 3 * devices - 1)
    start(copies)
    start(ghost_copies)
    await_blocks(part_in, part_s, part_r)
    contracted = part_out[member]
    for j in range(1, devices):
        contracted = contracted + part_in[senders[j]]
    whole[0] = contracted
    for side in range(2):
        for g, part in enumerate(ghost_rows_of(contracted, side)):
            qghost_out[side, :, g * LANES : (g + 1) * LANES] = part
    qcopies = [
        to_side(qghost_out.at[side], qghost_in.at[side], qghost_s, qghost_r, side)
        for side in range(2)
    ]
    start(qcopies)
    for copy in ghost_copies:
        copy.wait_recv()

    low, high = ghost_window(ghost_in, (0,), rows)
    own = [spread_row(charge[:, m * LANES : (m + 1) * LANES]) for m in range(atom_chunks)]
    chunks = low + own + high
    for m in range(atom_chunks):
        lanes = slice(m * LANES, (m + 1) * LANES)
        itself = ghosts + m * LANES + lax.broadcasted_iota(jnp.int32, (TILE, LANES), 1)
        for k in range(0, slots, TILE):
            index = near_ref[k : k + TILE, lanes]
            value = pick(chunks, index & (LANES - 1), index // LANES)
            weight[k : k + TILE, lanes] = jnp.where(index == itself, 0.0, value)

    cheap(0)
    gathered[0, me] = state[0] + (0.5 * inner_step) * kick[...]
    start([
        to_peer(gathered.at[0, me], gathered.at[0, me], all_s.at[0], all_r.at[0], j)
        for j in range(1, devices)
    ])
    for copy in qcopies:
        copy.wait_recv()
    learned(lambda c: ghost_window(qghost_in, (), c), 0)
    start(send_piece(0))
    await_blocks(gathered.at[0], all_s.at[0], all_r.at[0])
    await_blocks(piece.at[0], piece_s.at[0], piece_r.at[0])

    for step in range(1, NINNER + 1):
        every = gathered[step - 1].reshape(devices * rows, atoms)
        extra = None
        if step == 1:
            every = jnp.concatenate((every, all_pieces(0) * inverse), axis=0)
            fresh = dot(table_ref[0:rows, :], every)
        elif step < NINNER:
            fresh = dot(table_ref[0:rows, 0:full], every)
        else:
            both = dot(table_ref[0 : moved_row + TILE, 0:full], every)
            fresh = both[0:rows]
            extra = both[moved_row:]
            whole[0] = extra
        state[step] = fresh
        if step == 1:
            ghost_copies = send_ghosts(step, extra)
            start(ghost_copies)
            for copy in ghost_copies:
                copy.wait_recv()
        else:
            await_edges(step - 2)
            for side in range(2):
                edge = edge_in[step - 2, side].reshape(full, ghosts)
                ghost_in[step, side] = dot(table_ref[0 : moved_row + TILE, 0:full], edge)
        if step == NINNER:
            learned(lambda c: ghost_window(ghost_in, (step,), rows + c), 1)
            start(send_piece(1))
        cheap(step)
        if step < NINNER:
            gathered[step, me] = state[step] + inner_step * kick[...]
            start([
                to_peer(gathered.at[step, me], gathered.at[step, me],
                        all_s.at[step], all_r.at[step], j)
                for j in range(1, devices)
            ])
            for side in range(2):
                for at in range(0, rows, TILE):
                    block = gathered[step, me, at : at + TILE, :]
                    for g, part in enumerate(ghost_rows_of(block, side)):
                        edge_out[step - 1, side, at : at + TILE, g * LANES : (g + 1) * LANES] = part
                start([to_edge(step - 1, side, j) for j in range(devices)])
            await_blocks(gathered.at[step], all_s.at[step], all_r.at[step])

    await_blocks(piece.at[1], piece_s.at[1], piece_r.at[1])
    kick[...] = (state[NINNER] + (0.5 * inner_step) * kick[...]) * mass + dot(
        table_ref[spread_row_at : spread_row_at + rows, 0 : CB * TILE], all_pieces(1)
    )
    for component in range(3):
        at = row_of(component, 0, 0)
        new_pos_ref[component] = state[NINNER, at : at + per_device, :]
        at = row_of(component, 1, 0)
        new_mom_ref[component] = kick[at : at + per_device, :]
    for copy in sent:
        copy.wait_send()


def body(
    positions, momenta, neighbours, ghost_rows, species, species_scale, mass_table, w_in, w_out
):
    per_device, _, atoms = positions.shape
    slots = neighbours.shape[0]
    ghosts = ghost_rows.shape[0] // 2
    devices = lax.axis_size("bead")
    table = tables(devices, per_device)
    rows = -(-6 * per_device // TILE) * TILE
    cover = max(atoms // (devices // CB), LANES)
    vmem = pl.BlockSpec(memory_space=pltpu.VMEM)
    hbm = pl.BlockSpec(memory_space=pltpu.HBM)
    f32 = jnp.float32
    dma = pltpu.SemaphoreType.DMA
    operands = (
        positions.transpose(1, 0, 2), momenta.transpose(1, 0, 2), neighbours,
        ghost_rows.reshape(2, ghosts), species.reshape(1, atoms), species_scale.reshape(1, -1),
        mass_table.reshape(1, -1), w_in.T, w_out, table,
    )
    shape = jax.ShapeDtypeStruct(operands[0].shape, f32)
    new_positions, new_momenta = pl.pallas_call(
        cycle_kernel,
        name="cycle",
        out_shape=(shape, shape),
        in_specs=[hbm] * 10,
        out_specs=(vmem, vmem),
        scratch_shapes=[
            pltpu.VMEM((NINNER + 1, rows, atoms), f32),
            pltpu.VMEM((rows, atoms), f32),
            pltpu.VMEM((slots, atoms), f32),
            pltpu.VMEM((NINNER, devices, rows, atoms), f32),
            pltpu.VMEM((NINNER + 1, 2, rows + TILE, ghosts), f32),
            pltpu.VMEM((NINNER + 1, 2, rows + TILE, ghosts), f32),
            pltpu.VMEM((CB, TILE, atoms), f32),
            pltpu.VMEM((devices, TILE, atoms), f32),
            pltpu.VMEM((2, TILE, atoms), f32),
            pltpu.VMEM((2, TILE, ghosts), f32),
            pltpu.VMEM((2, TILE, ghosts), f32),
            pltpu.VMEM((2, devices, TILE, cover), f32),
            pltpu.VMEM((NINNER - 1, 2, rows, ghosts), f32),
            pltpu.VMEM((NINNER - 1, 2, devices, rows, ghosts), f32),
            *[pltpu.VMEM(operand.shape, operand.dtype) for operand in operands[:-1]],
            pltpu.VMEM(table.shape[1:], f32),
            dma((len(operands),)),
            dma((NINNER - 1, 2, devices)), dma((NINNER - 1, 2, devices)),
            dma((devices,)), dma((devices,)),
            dma((NINNER + 1, 2)), dma((NINNER + 1, 2)),
            dma((2,)), dma((2,)),
            dma((NINNER, devices)), dma((NINNER, devices)),
            dma((2, devices)), dma((2, devices)),
        ],
        compiler_params=pltpu.CompilerParams(
            collective_id=0, has_side_effects=True, vmem_limit_bytes=67043328
        ),
    )(*operands)
    return (new_positions.transpose(1, 0, 2), new_momenta.transpose(1, 0, 2))


def solution(mesh):
    in_specs = (
        P("bead", None, "space"),
        P("bead", None, "space"),
        P(None, "space"),
        P("space"),
        P("space"),
        P(),
        P(),
        P(),
        P(),
    )
    out_specs = (P("bead", None, "space"), P("bead", None, "space"))
    return jax.shard_map(body, mesh=mesh, in_specs=in_specs, out_specs=out_specs, check_vma=False)
```
